32 devices in a mesh: lat: 4 (over x, core), lon: 8 (over z, y).
Axes of the slice: x: 2, y: 2, z: 4, core: 2. Of those that a mesh axis runs over, the one named last changes fastest.
Arguments:
- queries: bfloat16 [8192, 2048], P(('lat', 'lon')), may hold values from -340 to 340
- keys: bfloat16 [8192, 2048], P(('lat', 'lon')), may hold values from -12 to 12
- values: bfloat16 [8192, 2048], P(('lat', 'lon')), may hold values from -6 to 6
- partners: int32 [32, 5], P(('lat', 'lon')), may hold values from -1 to 31, as said below
- out_weight: bfloat16 [2048, 2048], P(None, 'lat'), may hold values from -0.125 to 0.125
Outputs:
- projected: bfloat16 [8192, 2048], P(('lat', 'lon'))
The draws below stay inside these ranges and needn't reach their ends.
Inputs may be any that keep to these rules, and one draw needn't show every extreme that they name: `partners`: for each block, the first entries of its row are distinct blocks of its own band, none in its own sector or the two sectors beside it; the remaining entries are -1. In every band some block uses all 5 slots.
All inputs are finite; a program needn't handle non-finite values.
Results may differ from the reference program's by a relative error of at most 0.0095.
Values may be sent and summed in bfloat16 or wider, within the bound.
No kernel may reach another device: no remote copies, remote signals or barrier semaphores. Data moves between devices by JAX's collectives and lax.ppermute only.
A program may use at most 128 MiB of HBM per device.

```python
import math
import jax
import jax.numpy as jnp
from jax import lax

HEADS = 16
HEAD_DIM = 128
BLOCK = 256
D = 2048
SLOTS = 5
TOKENS = 8192
N_LAT = 4
N_LON = 8


def joint_draw(key):
    block_total = N_LAT * N_LON
    key_q, key_k = jax.random.split(jax.random.fold_in(key, 7), 2)
    draw_shape = (block_total, BLOCK, HEADS, HEAD_DIM)
    query_field = jax.random.truncated_normal(key_q, -6.0, 6.0, draw_shape, jnp.float32)
    key_field = jax.random.truncated_normal(key_k, -6.0, 6.0, draw_shape, jnp.float32)
    query_field = query_field.reshape(block_total * BLOCK, HEADS * HEAD_DIM)
    key_field = key_field.reshape(block_total * BLOCK, HEADS * HEAD_DIM)
    return (query_field, key_field)


def draw_queries(key, part):
    return joint_draw(key)[0].astype(jnp.bfloat16)


def draw_keys(key, part):
    return joint_draw(key)[1].astype(jnp.bfloat16)


def draw_partners(key, part):
    block_total = N_LAT * N_LON
    key_a, key_b, key_full, key_perm = jax.random.split(jax.random.fold_in(key, 13), 4)
    first_draw = jax.random.randint(key_a, (block_total,), 1, SLOTS + 1)
    second_draw = jax.random.randint(key_b, (block_total,), 1, SLOTS + 1)
    listed_count = jnp.minimum(first_draw, second_draw)
    full_sector = jax.random.randint(key_full, (N_LAT,), 0, N_LON)
    block_ids = jnp.arange(block_total)
    band_ids = block_ids // N_LON
    sector_ids = block_ids % N_LON
    listed_count = jnp.where(sector_ids == full_sector[band_ids], SLOTS, listed_count)
    subkeys = jax.random.split(key_perm, block_total)
    offsets = jax.vmap(lambda subkey: jax.random.permutation(subkey, SLOTS))(subkeys) + 2
    chosen = band_ids[:, None] * N_LON + (sector_ids[:, None] + offsets) % N_LON
    used = jnp.arange(SLOTS)[None, :] < listed_count[:, None]
    return jnp.where(used, chosen, -1).astype(jnp.int32)


def block_levels(own_key, extent, shards, least, high):
    level = 1.0
    for dim, parts in shards:
        draws = jax.random.uniform(jax.random.fold_in(jax.random.fold_in(own_key, 6), dim), (parts,), jnp.float32, least / len(shards), high / len(shards))
        level = level * jnp.repeat(jnp.exp(draws), extent[dim] // parts).reshape((-1,) + (1,) * (len(extent) - 1 - dim))
    return level


def scatter_about(rng, dims, deviation, most, shards=(), held_as=jnp.bfloat16):
    entries = deviation * jax.random.normal(rng, dims, jnp.float32)
    if shards:
        entries = entries * block_levels(rng, dims, shards, -0.22, 0.18)
    return jnp.clip(entries, -most, most).astype(held_as)


def setup_inputs(seed: int = 0) -> dict:
    seeds = jax.random.split(jax.random.key(seed), 6)
    return {
        "queries": draw_queries(jax.random.fold_in(seeds[5], 71), 0),
        "keys": draw_keys(jax.random.fold_in(seeds[5], 71), 0),
        "values": scatter_about(seeds[2], (TOKENS, D), 1.0, 6.0, ((0, 32),)),
        "partners": draw_partners(jax.random.fold_in(seeds[5], 71), 0),
        "out_weight": scatter_about(seeds[4], (D, D), D ** -0.5, 0.125, ((1, 4),)),
    }


very_low = -1e+30

def reference(queries, keys, values, partners, out_weight):
    block_total = N_LAT * N_LON
    score_scale = 1.0 / math.sqrt(HEAD_DIM)
    query_blocks = queries.reshape(block_total, BLOCK, HEADS, HEAD_DIM)
    key_bands = keys.reshape(N_LAT, N_LON * BLOCK, HEADS, HEAD_DIM)
    value_bands = values.reshape(N_LAT, N_LON * BLOCK, HEADS, HEAD_DIM)
    sectors = jnp.arange(N_LON, dtype=jnp.int32)

    def one_block(block_id):
        band_id = block_id // N_LON
        sector = block_id % N_LON
        listed_row = lax.dynamic_index_in_dim(partners, block_id, 0, keepdims=False)
        nearby = (sectors == sector) | (sectors == (sector + 1) % N_LON) | (sectors == (sector + N_LON - 1) % N_LON)
        named = jnp.any(listed_row[:, None] - band_id * N_LON == sectors[None, :], axis=0)
        member = jnp.repeat(nearby | named, BLOCK, total_repeat_length=N_LON * BLOCK)
        query_block = lax.dynamic_index_in_dim(query_blocks, block_id, 0, keepdims=False).astype(jnp.float32)
        key_band = lax.dynamic_index_in_dim(key_bands, band_id, 0, keepdims=False).astype(jnp.float32)
        value_band = lax.dynamic_index_in_dim(value_bands, band_id, 0, keepdims=False).astype(jnp.float32)
        scores = jnp.einsum('qhd,khd->hqk', query_block, key_band) * score_scale
        scores = jnp.where(member[None, None, :], scores, very_low)
        row_max = lax.optimization_barrier(jnp.max(scores, axis=-1, keepdims=True))
        weights = jnp.exp(scores - row_max)
        row_total = lax.optimization_barrier(jnp.sum(weights, axis=-1))
        rounded = weights.astype(jnp.bfloat16).astype(jnp.float32)
        mixture = jnp.einsum('hqk,khd->qhd', rounded, value_band)
        attended = mixture / row_total.T[:, :, None]
        return attended.reshape(BLOCK, HEADS * HEAD_DIM).astype(jnp.bfloat16)
    attended = lax.map(one_block, jnp.arange(block_total, dtype=jnp.int32))
    attended = attended.reshape(block_total * BLOCK, HEADS * HEAD_DIM)
    return jnp.dot(attended, out_weight, preferred_element_type=jnp.float32).astype(jnp.bfloat16)
```

```python
import functools
import math

import jax
import jax.numpy as jnp
from jax import lax
from jax.experimental import pallas as pl
from jax.experimental.pallas import tpu as pltpu
from jax.sharding import PartitionSpec as P

HEADS = 16
HEAD_DIM = 128
INFO_ROWS = 16
MIB = 1 << 20


very_low = -1e30
ANY = pl.BlockSpec(memory_space=pl.ANY)
VMEM = pl.BlockSpec(memory_space=pltpu.VMEM)
SMEM = pl.BlockSpec(memory_space=pltpu.SMEM)


def pack_kernel(lon, chunk, local_heads, place, partners, q, k, v, *rest):
    slabs, sems = rest[:-1], rest[-1]
    rows = q.shape[0]
    me = place[0]
    copies = []
    for s in range(lon):
        head = lax.bitwise_xor(me, s) * local_heads + chunk
        columns = pl.ds(pl.multiple_of(head * HEAD_DIM, HEAD_DIM), HEAD_DIM)
        for a, source in enumerate((q, k, v)):
            copy = pltpu.make_async_copy(
                source.at[:, columns], slabs[s].at[pl.ds(a * rows, rows)], sems.at[3 * s + a]
            )
            copy.start()
            copies.append(copy)
    lane = lax.broadcasted_iota(jnp.int32, (INFO_ROWS, HEAD_DIM), 1)
    info = jnp.where(lane == 1, me, 0)
    info = jnp.where(lane == 2, lax.rem(me + 1, lon), info)
    info = jnp.where(lane == 3, lax.rem(me + lon - 1, lon), info)
    count = jnp.int32(3)
    for j in range(partners.shape[1]):
        named = partners[0, j]
        count = count + jnp.where(named >= 0, 1, 0)
        info = jnp.where(lane == 4 + j, jnp.maximum(named - place[1], 0), info)
    info = jnp.where(lane == 0, count, info).astype(jnp.float32).astype(jnp.bfloat16)
    for s in range(lon):
        slabs[s][pl.ds(3 * rows, INFO_ROWS), :] = info
    for copy in copies:
        copy.wait()


def pack(lon, chunk, local_heads, place, partners, q, k, v):
    rows = q.shape[0]
    slab = jax.ShapeDtypeStruct((3 * rows + INFO_ROWS, HEAD_DIM), jnp.bfloat16)
    return pl.pallas_call(
        functools.partial(pack_kernel, lon, chunk, local_heads),
        out_shape=[slab] * lon,
        in_specs=[SMEM, SMEM, ANY, ANY, ANY],
        out_specs=[VMEM] * lon,
        scratch_shapes=[pltpu.SemaphoreType.DMA((3 * lon,))],
        compiler_params=pltpu.CompilerParams(vmem_limit_bytes=16 * MIB),
        cost_estimate=pl.CostEstimate(
            flops=0, transcendentals=0, bytes_accessed=2 * lon * 3 * rows * HEAD_DIM * 2
        ),
        name="pack",
    )(place, partners, q, k, v)


def attend_kernel(lon, low, high, place, *rest):
    rows = (rest[0].shape[0] - INFO_ROWS) // 3
    slabs, outs = rest[:lon], rest[lon : lon + high - low]
    held, v_turned, scores, results, info_vmem, info, sems, info_sem = rest[lon + high - low :]
    me = place[0]
    factor = math.log2(math.e) / math.sqrt(HEAD_DIM)
    copies = [pltpu.make_async_copy(slabs[s], held.at[s], sems.at[s]) for s in range(lon)]
    for copy in copies:
        copy.start()
    for copy in copies:
        copy.wait()

    def turn(t, _):
        v_turned[t] = held[t, pl.ds(2 * rows, rows), :].T
        row = held[t, pl.ds(3 * rows, INFO_ROWS), :].astype(jnp.float32).astype(jnp.int32)
        info_vmem[pl.ds(t, 1), :] = row[0:1, :]
        return 0

    lax.fori_loop(0, lon, turn, 0)
    to_scalars = pltpu.make_async_copy(info_vmem, info, info_sem)
    to_scalars.start()
    to_scalars.wait()

    def one_query(s, _):
        query = held[s, pl.ds(0, rows), :]
        count = info[s, 0]

        def score(j, top):
            t = lax.bitwise_xor(me, info[s, 1 + j])
            block = lax.dot_general(
                held[t, pl.ds(rows, rows), :],
                query,
                (((1,), (1,)), ((), ())),
                preferred_element_type=jnp.float32,
            )
            scores[j] = block
            return jnp.maximum(top, jnp.max(block.reshape(rows // 8, 8, rows), axis=0))

        top = lax.fori_loop(0, count, score, jnp.full((8, rows), very_low, jnp.float32))
        shift = jnp.max(top, axis=0, keepdims=True) * factor

        def mix(j, carry):
            total, mixture = carry
            t = lax.bitwise_xor(me, info[s, 1 + j])
            weights = jnp.exp2(scores[j] * factor - shift)
            total = total + jnp.sum(weights.reshape(rows // 8, 8, rows), axis=0)
            mixture = mixture + jnp.dot(
                v_turned[t], weights.astype(jnp.bfloat16), preferred_element_type=jnp.float32
            )
            return total, mixture

        total, mixture = lax.fori_loop(
            0,
            count,
            mix,
            (jnp.zeros((8, rows), jnp.float32), jnp.zeros((HEAD_DIM, rows), jnp.float32)),
        )
        total = jnp.sum(total, axis=0, keepdims=True)
        results[s - low] = (mixture * (1.0 / total)).T.astype(jnp.bfloat16)
        return 0

    lax.fori_loop(low, high, one_query, 0)
    for i, out in enumerate(outs):
        out[...] = results[i]


def attend(lon, low, high, most, place, slabs):
    slab_rows = slabs[0].shape[0]
    rows = (slab_rows - INFO_ROWS) // 3
    flops = (high - low) * most * rows * rows * HEAD_DIM * 4
    return pl.pallas_call(
        functools.partial(attend_kernel, lon, low, high),
        out_shape=[jax.ShapeDtypeStruct((rows, HEAD_DIM), jnp.bfloat16)] * (high - low),
        in_specs=[SMEM] + [ANY] * lon,
        out_specs=[VMEM] * (high - low),
        scratch_shapes=[
            pltpu.VMEM((lon, slab_rows, HEAD_DIM), jnp.bfloat16),
            pltpu.VMEM((lon, HEAD_DIM, rows), jnp.bfloat16),
            pltpu.VMEM((most, rows, rows), jnp.float32),
            pltpu.VMEM((high - low, rows, HEAD_DIM), jnp.bfloat16),
            pltpu.VMEM((lon, HEAD_DIM), jnp.int32),
            pltpu.SMEM((lon, HEAD_DIM), jnp.int32),
            pltpu.SemaphoreType.DMA((lon,)),
            pltpu.SemaphoreType.DMA,
        ],
        compiler_params=pltpu.CompilerParams(vmem_limit_bytes=24 * MIB),
        cost_estimate=pl.CostEstimate(
            flops=flops, transcendentals=flops // (4 * HEAD_DIM), bytes_accessed=2 * lon * slab_rows * HEAD_DIM
        ),
        name="attend",
    )(place, *slabs)


def project_kernel(lon, lat, chunk, first, last, place, *rest):
    pieces, shards = rest[:lon], rest[lon : lon + lat]
    rest = rest[lon + lat :]
    if first:
        out, attended, held, sems = rest
    else:
        so_far, out, attended, held, sems = rest
    me, my_lat = place[0], place[2]
    columns = held.shape[-1]
    copies = [pltpu.make_async_copy(shards[t].at[:, chunk], held.at[t], sems.at[t]) for t in range(lat)]
    for copy in copies:
        copy.start()
    for s in range(lon):
        block = lax.bitwise_xor(me, s)
        attended[:, pl.ds(pl.multiple_of(block * HEAD_DIM, HEAD_DIM), HEAD_DIM)] = pieces[s][...]
    for t in range(lat):
        copies[t].wait()
        into = pl.ds(pl.multiple_of(lax.bitwise_xor(my_lat, t) * columns, columns), columns)
        product = jnp.dot(
            attended[...],
            held[t].reshape(lon * HEAD_DIM, columns),
            preferred_element_type=jnp.float32,
        )
        if not first:
            product = product + so_far[:, into]
        out[:, into] = product.astype(out.dtype)


def project(lon, lat, chunk, place, pieces, shards, so_far, last):
    rows = pieces[0].shape[0]
    columns = shards[0].shape[-1]
    first = so_far is None
    dtype = jnp.bfloat16 if last else jnp.float32
    return pl.pallas_call(
        functools.partial(project_kernel, lon, lat, chunk, first, last),
        out_shape=jax.ShapeDtypeStruct((rows, lat * columns), dtype),
        in_specs=[SMEM] + [VMEM] * lon + [ANY] * lat + ([] if first else [VMEM]),
        out_specs=VMEM,
        scratch_shapes=[
            pltpu.VMEM((rows, lon * HEAD_DIM), jnp.bfloat16),
            pltpu.VMEM((lat, lon, HEAD_DIM, columns), jnp.bfloat16),
            pltpu.SemaphoreType.DMA((lat,)),
        ],
        compiler_params=pltpu.CompilerParams(vmem_limit_bytes=24 * MIB),
        cost_estimate=pl.CostEstimate(
            flops=2 * rows * lon * HEAD_DIM * lat * columns,
            transcendentals=0,
            bytes_accessed=2 * lon * HEAD_DIM * lat * columns,
        ),
        name="project",
    )(place, *pieces, *shards, *([] if first else [so_far]))


def per_device(queries, keys, values, partners, out_weight):
    lon, lat = lax.axis_size("lon"), lax.axis_size("lat")
    me, my_lat = lax.axis_index("lon"), lax.axis_index("lat")
    place = jnp.stack([me, my_lat * lon, my_lat]).astype(jnp.int32)
    local_heads = HEADS // lon
    most = min(lon, 3 + partners.shape[1])
    half = lon // 2

    def swap(x, axis, size, s):
        return lax.ppermute(x, axis, [(i, i ^ s) for i in range(size)])

    def exchange(pieces):
        got = {0: pieces[0]}
        for s in range(lon - 1, 0, -1):
            got[s] = swap(pieces[s], "lon", lon, s)
        return [got[s] for s in range(lon)]

    received = []
    for chunk in range(local_heads):
        slabs = pack(lon, chunk, local_heads, place, partners, queries, keys, values)
        received.append(exchange(slabs))

    shards = {0: out_weight.reshape(lon, local_heads, HEAD_DIM, out_weight.shape[1])}
    step = lat // 2
    while step:
        for t in list(shards):
            shards[t ^ step] = swap(shards[t], "lat", lat, step)
        step //= 2
    shards = [shards[t] for t in range(lat)]

    returned = []
    for chunk in range(local_heads):
        far = attend(lon, half, lon, most, place, received[chunk])
        near = attend(lon, 0, half, most, place, received[chunk])
        returned.append(exchange(list(near) + list(far)))

    so_far = None
    for chunk in range(local_heads):
        so_far = project(
            lon, lat, chunk, place, returned[chunk], shards, so_far, chunk == local_heads - 1
        )
    return so_far


def solution(mesh):
    return jax.shard_map(
        per_device,
        mesh=mesh,
        in_specs=(
            P(("lat", "lon"), None),
            P(("lat", "lon"), None),
            P(("lat", "lon"), None),
            P(("lat", "lon"), None),
            P(None, "lat"),
        ),
        out_specs=P(("lat", "lon"), None),
        check_vma=False,
    )
```
